256 devices in a mesh: af: 128 (over x, y, z), sa: 2 (over core).
Axes of the slice: x: 4, y: 4, z: 8, core: 2. Of those that a mesh axis runs over, the one named last changes fastest.
Arguments:
- series: float32 [8, 2097152], P('sa', 'af'), parts along dimension 0, may hold values from -48 to 48
- tapers: float32 [10, 2097152], P(None, 'af'), may hold values from -16 to 16
- concentration: float32 [10], replicated, may hold values from 0.2 to 0.95
- qi_weights: float32 [4, 10, 10], replicated, may hold values from -0.625 to 0.625
Outputs:
- spectrum: float32 [8, 128, 16384], P('sa', 'af'), parts along dimension 0
- qi_terms: float32 [8, 4, 128, 16384], P('sa', None, 'af'), parts along dimension 0
The draws below stay inside these ranges and needn't reach their ends.
There are 2 independent parts, one for each index of `sa`. The reference program is written for one: setup_inputs(seed, part) draws one part's arguments, and reference() takes and returns one part's arrays. A program takes and returns all parts, laid end to end along the dimension named above; an argument that names none is the same for every part. Nothing has to cross between parts.
All inputs are finite; a program needn't handle non-finite values.
Results may differ from the reference program's by a relative error of at most 0.0001.
Values sent between devices are 32-bit elements; how exact they have to be, the bound alone decides.
No kernel may reach another device: no remote copies, remote signals or barrier semaphores. Data moves between devices by JAX's collectives and lax.ppermute only.
A program may use at most 64 MiB of HBM per device.

```python
import math
import jax
import jax.numpy as jnp
from jax import lax

K = 10
L = 4
ITERS = 3
SERIES = 4
TIME_DEV = 16384
SAMPLES = 2097152
N_AF = 128


def draw_series(key, part):
    noise_key = jax.random.fold_in(key, 17)
    cycle_key = jax.random.fold_in(key, 29)
    time_frac = jnp.arange(SAMPLES, dtype=jnp.float32) / SAMPLES
    period = SAMPLES // TIME_DEV
    noise_part = jnp.clip(jax.random.normal(noise_key, (SERIES, SAMPLES), jnp.float32), -6.0, 6.0)
    memory_coef = 0.9
    envelope = jnp.exp(math.log(3.0) * time_frac)
    cycle_part = jnp.clip(jax.random.normal(cycle_key, (SERIES, TIME_DEV), jnp.float32), -4.0, 4.0)
    strength = 3.0
    shifted = jnp.roll(noise_part, 1, axis=1)
    repeated = jnp.tile(cycle_part, (1, period))
    return ((noise_part + memory_coef * shifted) * envelope[None, :] + strength * repeated).astype(jnp.float32)


def draw_tapers(key, part):
    coef_key = jax.random.fold_in(key, 41)
    rough_key = jax.random.fold_in(key, 43)
    harmonic_count = K + 2
    positions = (jnp.arange(SAMPLES, dtype=jnp.float32) + 1.0) / (SAMPLES + 1)
    harmonics = jnp.arange(1, harmonic_count + 1, dtype=jnp.float32)
    sine_basis = jnp.sin(math.pi * harmonics[:, None] * positions[None, :])
    coeffs = jnp.clip(jax.random.normal(coef_key, (K, harmonic_count), jnp.float32), -3.0, 3.0) * math.sqrt(2.0 / harmonic_count)
    rough_part = jnp.clip(jax.random.normal(rough_key, (K, SAMPLES), jnp.float32), -4.0, 4.0) * 0.15
    smooth = jnp.dot(coeffs, sine_basis, precision=lax.Precision.HIGHEST)
    return (smooth + rough_part).astype(jnp.float32)


def noise(own_key, extent, width, reach, kind=jnp.bfloat16):
    return jnp.clip(width * jax.random.normal(own_key, extent, jnp.float32), -reach, reach).astype(kind)


def setup_inputs(seed: int = 0, part: int = 0) -> dict:
    keys = jax.random.split(jax.random.key(seed), 5)
    part_keys = jax.random.split(jax.random.fold_in(keys[4], part), 5)
    return {
        "series": draw_series(jax.random.fold_in(jax.random.fold_in(keys[4], part), 71), part),
        "tapers": draw_tapers(jax.random.fold_in(keys[4], 71), part),
        "concentration": jnp.clip(jax.random.uniform(keys[2], (K,), jnp.float32, 0.2, 0.95), 0.2, 0.95),
        "qi_weights": noise(keys[3], (L, K, K), (K * K) ** -0.5, 0.625, jnp.float32),
    }


def reference(series, tapers, concentration, qi_weights):
    highest = lax.Precision.HIGHEST
    retained = concentration[:, None]
    unit_scale = 1.0 / math.sqrt(SAMPLES)
    spectra = []
    term_list = []
    for series_index in range(SERIES):
        scaled = series[series_index] * unit_scale
        coeffs = jnp.fft.fft(tapers * scaled[None, :], axis=1)
        coeffs = coeffs.reshape(K, TIME_DEV, N_AF).transpose(0, 2, 1).reshape(K, SAMPLES)
        real_part = jnp.real(coeffs)
        imag_part = jnp.imag(coeffs)
        powers = real_part * real_part + imag_part * imag_part
        per_term = []
        for term_index in range(L):
            mixed_re = jnp.dot(qi_weights[term_index], real_part, precision=highest)
            mixed_im = jnp.dot(qi_weights[term_index], imag_part, precision=highest)
            per_term.append(lax.optimization_barrier(jnp.sum(real_part * mixed_re + imag_part * mixed_im, axis=0)))
        estimate = 0.5 * (powers[0] + powers[1])
        for sweep_index in range(ITERS):
            variance = jnp.mean(estimate)
            weight = retained / (retained * estimate[None, :] + (1.0 - retained) * variance) ** 2
            estimate = lax.optimization_barrier(jnp.sum(weight * powers, axis=0)) / lax.optimization_barrier(jnp.sum(weight, axis=0))
        spectra.append(estimate.reshape(N_AF, TIME_DEV))
        term_list.append(jnp.stack(per_term).reshape(L, N_AF, TIME_DEV))
    return (jnp.stack(spectra), jnp.stack(term_list))
```

```python
import functools
import math

import jax
import jax.numpy as jnp
import numpy as np
from jax import lax
from jax.experimental import pallas as pl
from jax.experimental.pallas import tpu as pltpu
from jax.sharding import Mesh
from jax.sharding import PartitionSpec as P

ITERS = 3
AF = ("af_0", "af_1", "af_2")
R = 128
HALF = 64
INNER = R * R
ROWS = R + 8
K = 10
L = 4
F32 = jnp.float32
BF16 = jnp.bfloat16
VMEM = pl.BlockSpec(memory_space=pltpu.VMEM)
SMEM = pl.BlockSpec(memory_space=pltpu.SMEM)
PARAMS = pltpu.CompilerParams(vmem_limit_bytes=24 << 20)


def split(x):
    hi = x.astype(BF16)
    lo = (x - hi.astype(F32)).astype(BF16)
    return hi, lo


def dot3(a, b):
    left = jnp.concatenate([a[0], a[0], a[1]], axis=1)
    right = jnp.concatenate([b[0], b[1], b[0]], axis=0)
    return jnp.dot(left, right, preferred_element_type=F32)


def host_split(x):
    hi = x.astype(np.float32).astype(BF16)
    lo = (x - hi.astype(np.float64)).astype(np.float32).astype(BF16)
    return hi, lo


def first_table(scale):
    dest = np.arange(R)[:, None]
    angle = 2.0 * np.pi * (dest * np.arange(R)[None, :] % R) / R
    real = np.cos(angle)
    imag = -np.sin(angle)
    imag[0] = imag[HALF] = real[HALF]
    real[HALF] = real[0]
    both = [np.concatenate([real[g * HALF :][:HALF], imag[g * HALF :][:HALF]]) for g in (0, 1)]
    return host_split(np.stack(both) * scale)


def last_table():
    angle = 2.0 * np.pi * (np.arange(R)[:, None] * np.arange(R)[None, :] % R) / R
    cos, sin = np.cos(angle), -np.sin(angle)
    return host_split(np.block([[cos, sin], [-sin, cos]]))


def pack_kernel(series_ref, tapers_ref, out_ref):
    total = jnp.zeros((4, R), F32)
    for d in range(R):
        cols = pl.ds(d * R, R)
        x = series_ref[:, cols]
        t = tapers_ref[0:2, cols]
        t = t * t
        total = total + (t[0:1] + t[1:2]) * (x * x)
    power = jnp.sum(total, axis=1, keepdims=True)
    lane = lax.broadcasted_iota(jnp.int32, (4, R), 1)
    row = lax.broadcasted_iota(jnp.int32, (4, R), 0)
    extra = jnp.sum(jnp.where(lane == row, power, 0.0), axis=0, keepdims=True)
    extra = jnp.concatenate([extra, jnp.zeros((1, R), F32)], axis=0)
    for d in range(R):
        cols = pl.ds(d * R, R)
        out_ref[d, 0:K, :] = tapers_ref[:, cols]
        out_ref[d, K : K + 4, :] = series_ref[:, cols]
        out_ref[d, K + 4 :, :] = extra


def first_kernel(got_ref, mhi_ref, mlo_ref, out_ref, power_ref, taper_ref):
    def plane(i):
        return got_ref[pl.ds(i, R, stride=16), :]

    for k in range(K):
        taper_ref[k] = plane(k)
    power_ref[...] = jnp.sum(plane(K + 4), axis=0, keepdims=True)
    for g in range(2):
        table = (mhi_ref[g], mlo_ref[g])
        for s in range(2):
            x = plane(K + 2 * g + s)
            for k in range(0, K, 2):
                y = jnp.concatenate([taper_ref[k] * x, taper_ref[k + 1] * x], axis=1)
                res = dot3(table, split(y))
                for h in range(2):
                    at = g * HALF * 4 * K + s * K + k + h
                    part = res[:, h * R : (h + 1) * R]
                    out_ref[pl.ds(at, HALF, stride=4 * K), :] = part[:HALF]
                    out_ref[pl.ds(at + 2 * K, HALF, stride=4 * K), :] = part[HALF:]


def refine(estimate, variance, powers, conc_ref):
    num = jnp.zeros_like(estimate)
    den = jnp.zeros_like(estimate)
    for k in range(K):
        kept = conc_ref[k]
        base = kept * estimate + (1.0 - kept) * variance
        weight = kept / (base * base)
        num = num + weight * powers[k]
        den = den + weight
    return num / den


def arrange(x, route_ref, turn_ref):
    row = lax.broadcasted_iota(jnp.int32, (R, R), 0)
    col = lax.broadcasted_iota(jnp.int32, (R, R), 1)
    flip = jnp.where(row + col == R - 1, 1.0, 0.0).astype(BF16)
    dot = functools.partial(jnp.dot, preferred_element_type=F32)
    route = route_ref[0 : 2 * R]
    extra = route_ref[2 * R : 2 * R + 16].astype(F32)[0:1]
    own, send = [], []
    last = []
    for i, plane in enumerate(x):
        turned = plane[:R].T
        last.append(plane[R:].T[:, 0:1])
        hi, lo = split(turned)
        turn_ref[:, 2 * i * R : (2 * i + 1) * R] = hi
        turn_ref[:, (2 * i + 1) * R : (2 * i + 2) * R] = lo
    for i in range(len(x)):
        both = turn_ref[:, 2 * i * R : (2 * i + 2) * R]
        back = dot(flip, both).astype(BF16)
        left = [both[:, :R], back[:, :R], both[:, R:], back[:, R:]]
        out = dot(jnp.concatenate(left, axis=1), jnp.concatenate([route, route], axis=0))
        out = out + last[i] * extra
        own.append(out[:, :R])
        send.append(out[:, R:])
    return own, send


def block(b):
    return pl.ds(pl.multiple_of(b * 8, 8), 8)


def counted(estimate, b, special):
    row = b * 8 + lax.broadcasted_iota(jnp.int32, (8, R), 0)
    single = jnp.logical_and(special == 1, jnp.logical_or(row == 0, row == R))
    times = jnp.where(single, 1.0, jnp.where(row < R, 2.0, 0.0))
    return jnp.where(times > 0.0, estimate * times, 0.0)


def share_sums(sums_ref, part_ref, totals):
    lane = lax.broadcasted_iota(jnp.int32, sums_ref.shape, 1)
    out = jnp.zeros(sums_ref.shape, F32)
    for s in range(2):
        out = jnp.where(lane == 2 * part_ref[0] + s, jnp.sum(totals[s]), out)
    sums_ref[...] = out


def read_mean(sums_ref, part_ref, s, scale):
    sums = sums_ref[...]
    lane = lax.broadcasted_iota(jnp.int32, sums.shape, 1)
    return jnp.sum(jnp.where(lane == 2 * part_ref[0] + s, sums, 0.0)) * scale


def second_kernel(
    length_all, part_ref, conc_ref, got_ref, power_ref, w1_ref, tw_ref, ehi_ref, elo_ref,
    xr_ref, xi_ref, powers_ref, est_ref, sums_ref,
):
    means = [read_mean(power_ref, part_ref, s, 0.5 / length_all) for s in range(2)]
    table = split(w1_ref[...])
    last = (ehi_ref[...], elo_ref[...])
    cos, sin = tw_ref[0], tw_ref[1]

    def plane(i):
        return got_ref[pl.ds(i, R, stride=4 * K), :]

    for a in range(0, 2 * K, 2):
        left = jnp.concatenate([plane(a), plane(2 * K + a)], axis=0)
        right = jnp.concatenate([plane(a + 1), plane(2 * K + a + 1)], axis=0)
        mid = dot3(table, split(jnp.concatenate([left, right], axis=1)))
        rows = []
        for h in range(2):
            re = mid[:ROWS, h * R : (h + 1) * R]
            im = mid[ROWS:, h * R : (h + 1) * R]
            rows.append(jnp.concatenate([re * cos - im * sin, re * sin + im * cos], axis=1))
        out = dot3(split(jnp.concatenate(rows, axis=0)), last)
        for h in range(2):
            re = out[h * ROWS : (h + 1) * ROWS, :R]
            im = out[h * ROWS : (h + 1) * ROWS, R:]
            xr_ref[a + h] = re
            xi_ref[a + h] = im
            powers_ref[a + h] = re * re + im * im

    def rest(b, totals):
        rows = block(b)
        totals = list(totals)
        for s in range(2):
            powers = [powers_ref[s * K + k, rows, :] for k in range(K)]
            estimate = refine(0.5 * (powers[0] + powers[1]), means[s], powers, conc_ref)
            est_ref[s, rows, :] = estimate
            totals[s] = totals[s] + counted(estimate, b, part_ref[1])
        return tuple(totals)

    zero = jnp.zeros((8, R), F32)
    share_sums(sums_ref, part_ref, lax.fori_loop(0, ROWS // 8, rest, (zero, zero)))


def inverse_kernel(qi_ref, xr_ref, xi_ref, route_ref, own_ref, send_ref, out_ref, pair_ref, turn_ref):
    at = 0
    for j in range(K):
        for k in range(j, K):
            for l in range(L):
                value = qi_ref[l, j, k]
                value = value if j == k else value + qi_ref[l, k, j]
                pair_ref[at] = jnp.full((8, R), value, F32)
                at += 1

    def step(b, carry):
        rows = block(b)
        re = [xr_ref[i, rows, :] for i in range(2 * K)]
        im = [xi_ref[i, rows, :] for i in range(2 * K)]
        acc = [[None] * L for _ in range(2)]
        at = 0
        for j in range(K):
            for k in range(j, K):
                cross = [
                    re[s * K + j] * re[s * K + k] + im[s * K + j] * im[s * K + k] for s in range(2)
                ]
                for l in range(L):
                    pair = pair_ref[at]
                    at += 1
                    for s in range(2):
                        term = pair * cross[s]
                        acc[s][l] = term if acc[s][l] is None else acc[s][l] + term
        for s in range(2):
            for l in range(L):
                out_ref[s * L + l, rows, :] = acc[s][l]
        return carry

    lax.fori_loop(0, ROWS // 8, step, 0)
    own, send = arrange([out_ref[i] for i in range(2 * L)], route_ref, turn_ref)
    for i in range(2 * L):
        own_ref[i], send_ref[i] = own[i], send[i]


def refine_kernel(length_all, part_ref, conc_ref, got_ref, powers_ref, est_ref, new_ref, sums_ref):
    means = [read_mean(got_ref, part_ref, s, 1.0 / length_all) for s in range(2)]

    def step(b, totals):
        rows = block(b)
        totals = list(totals)
        for s in range(2):
            powers = [powers_ref[s * K + k, rows, :] for k in range(K)]
            estimate = refine(est_ref[s, rows, :], means[s], powers, conc_ref)
            new_ref[s, rows, :] = estimate
            totals[s] = totals[s] + counted(estimate, b, part_ref[1])
        return tuple(totals)

    zero = jnp.zeros((8, R), F32)
    share_sums(sums_ref, part_ref, lax.fori_loop(0, ROWS // 8, step, (zero, zero)))


def finish_kernel(
    length_all, part_ref, conc_ref, got_ref, powers_ref, est_ref, route_ref, own_ref, send_ref,
    new_ref, turn_ref,
):
    means = [read_mean(got_ref, part_ref, s, 1.0 / length_all) for s in range(2)]

    def step(b, carry):
        rows = block(b)
        for s in range(2):
            powers = [powers_ref[s * K + k, rows, :] for k in range(K)]
            new_ref[s, rows, :] = refine(est_ref[s, rows, :], means[s], powers, conc_ref)
        return carry

    lax.fori_loop(0, ROWS // 8, step, 0)
    own, send = arrange([new_ref[s] for s in range(2)], route_ref, turn_ref)
    for s in range(2):
        own_ref[s], send_ref[s] = own[s], send[s]


def merge_kernel(part_ref, mine_ref, theirs_ref, out_ref):
    half = mine_ref.shape[0]
    for g in range(2):

        @pl.when(part_ref[0] == g)
        def _():
            out_ref[g * half : (g + 1) * half] = mine_ref[...]
            out_ref[(1 - g) * half : (2 - g) * half] = theirs_ref[...]


def exchange(x):
    return lax.all_to_all(x, AF, split_axis=0, concat_axis=0, tiled=True)


def tables(q, special, length_all):
    row = lax.broadcasted_iota(jnp.int32, (ROWS, R), 0)
    col = lax.broadcasted_iota(jnp.int32, (ROWS, R), 1)
    upper = jnp.logical_and(row >= HALF, row < R)
    halves = jnp.where(row < HALF, R * row, jnp.where(row < R, R * (row - HALF) + HALF, R * HALF))
    phase = col * jnp.where(special, halves, R * row + q)
    angle = (phase % INNER).astype(F32) * (2.0 * math.pi / INNER)
    re, im = jnp.cos(angle), -jnp.sin(angle)
    ordinary = jnp.logical_and(jnp.logical_not(special), row < R)
    from_imag = jnp.logical_and(special, upper)
    from_real = jnp.logical_or(
        ordinary, jnp.logical_and(special, jnp.logical_or(row < HALF, row == R))
    )
    a = jnp.where(from_real, re, 0.0)
    c = jnp.where(from_real, im, 0.0)
    b = jnp.where(ordinary, -im, jnp.where(from_imag, re, 0.0))
    d = jnp.where(ordinary, re, jnp.where(from_imag, im, 0.0))
    first = jnp.concatenate([jnp.concatenate([a, b], axis=1), jnp.concatenate([c, d], axis=1)])
    angle = phase.astype(F32) * (2.0 * math.pi / length_all)
    return first, jnp.stack([jnp.cos(angle), -jnp.sin(angle)])


def route_table(q, special):
    row = lax.broadcasted_iota(jnp.int32, (2 * R + 16, 2 * R), 0)
    col = lax.broadcasted_iota(jnp.int32, (2 * R + 16, 2 * R), 1)
    c = col % R
    send = col >= R
    row_0 = jnp.where(c < HALF, c, jnp.where(c == HALF, 2 * R, R + R - c))
    row_64 = jnp.where(c < HALF, HALF + c, R + HALF + R - 1 - c)
    plain = jnp.where(send, R + R - 1 - c, c)
    source = jnp.where(special, jnp.where(send == (q == 0), row_64, row_0), plain)
    return (row == source).astype(BF16)


def local(series, tapers, concentration, qi_weights):
    length_all = series.shape[1] * R
    q = lax.axis_index(AF)
    group = (q >= HALF).astype(jnp.int32)
    special = (q % HALF) == 0
    part = jnp.stack([group, special.astype(jnp.int32)])
    shape = jax.ShapeDtypeStruct

    packed = pl.pallas_call(
        pack_kernel,
        out_shape=shape((R, 16, R), F32),
        in_specs=[VMEM] * 2,
        out_specs=VMEM,
        name="pack",
        compiler_params=PARAMS,
    )(series, tapers)
    got = exchange(packed)

    first, tw = tables(q, special, length_all)
    route = route_table(q, special)
    mhi, mlo = first_table(1.0 / math.sqrt(length_all))
    spread, power = pl.pallas_call(
        first_kernel,
        out_shape=(shape((R * 4 * K, R), F32), shape((1, R), F32)),
        in_specs=[VMEM] * 3,
        out_specs=(VMEM, VMEM),
        scratch_shapes=[pltpu.VMEM((K, R, R), F32)],
        name="first",
        compiler_params=PARAMS,
    )(got.reshape(R * 16, R), jnp.asarray(mhi), jnp.asarray(mlo))
    got = exchange(spread.reshape(R, 4 * K, R)).reshape(R * 4 * K, R)

    ehi, elo = last_table()
    spectra = shape((2 * K, ROWS, R), F32)
    estimates = shape((2, ROWS, R), F32)
    totals = shape((R, 8), F32)
    xr, xi, powers, est, sums = pl.pallas_call(
        functools.partial(second_kernel, length_all),
        out_shape=(spectra, spectra, spectra, estimates, totals),
        in_specs=[SMEM] * 2 + [VMEM] * 6,
        out_specs=(VMEM,) * 5,
        name="second",
        compiler_params=PARAMS,
    )(part, concentration, got, power, first, tw, jnp.asarray(ehi), jnp.asarray(elo))

    sums = exchange(sums)
    parts = shape((2 * L, R, R), F32)
    own_qi, send_qi = pl.pallas_call(
        inverse_kernel,
        out_shape=(parts, parts),
        in_specs=[SMEM] + [VMEM] * 3,
        out_specs=(VMEM,) * 2,
        scratch_shapes=[
            pltpu.VMEM((2 * L, ROWS, R), F32),
            pltpu.VMEM((L * K * (K + 1) // 2, 8, R), F32),
            pltpu.VMEM((R, 4 * L * R), BF16),
        ],
        cost_estimate=pl.CostEstimate(flops=10**9, bytes_accessed=10**7, transcendentals=0),
        name="inverse",
        compiler_params=PARAMS,
    )(qi_weights, xr, xi, route)

    sums, own_qi, send_qi = lax.optimization_barrier((sums, own_qi, send_qi))
    partner = [(i, HALF - i if i % HALF == 0 else R - i) for i in range(R)]
    got_qi = lax.ppermute(send_qi, AF, partner)

    est, sums = pl.pallas_call(
        functools.partial(refine_kernel, length_all),
        out_shape=(estimates, totals),
        in_specs=[SMEM] * 2 + [VMEM] * 3,
        out_specs=(VMEM,) * 2,
        name="refine",
        compiler_params=PARAMS,
    )(part, concentration, sums, powers, est)
    sums = exchange(sums)

    def merge(mine, theirs):
        return pl.pallas_call(
            merge_kernel,
            out_shape=shape((2 * mine.shape[0], R, R), F32),
            in_specs=[SMEM] + [VMEM] * 2,
            out_specs=VMEM,
            name="merge",
            compiler_params=PARAMS,
        )(part, mine, theirs)

    qi_out = merge(own_qi, got_qi)
    sums, qi_out = lax.optimization_barrier((sums, qi_out))
    parts = shape((2, R, R), F32)
    own, send = pl.pallas_call(
        functools.partial(finish_kernel, length_all),
        out_shape=(parts, parts),
        in_specs=[SMEM] * 2 + [VMEM] * 4,
        out_specs=(VMEM,) * 2,
        scratch_shapes=[pltpu.VMEM((2, ROWS, R), F32), pltpu.VMEM((R, 4 * R), BF16)],
        name="finish",
        compiler_params=PARAMS,
    )(part, concentration, sums, powers, est, route)
    got_est = lax.ppermute(send, AF, partner)
    return merge(own, got_est).reshape(4, 1, INNER), qi_out.reshape(4, L, 1, INNER)


def solution(mesh):
    torus = Mesh(mesh.devices.reshape(4, 4, 8, mesh.shape["sa"]), AF + ("sa",))
    in_specs = (P("sa", AF), P(None, AF), P(), P())
    out_specs = (P("sa", AF, None), P("sa", None, AF, None))
    return jax.shard_map(local, mesh=torus, in_specs=in_specs, out_specs=out_specs, check_vma=False)
```

```python
import functools
import math

import jax
import jax.numpy as jnp
import numpy as np
from jax import lax
from jax.experimental import pallas as pl
from jax.experimental.pallas import tpu as pltpu
from jax.sharding import Mesh
from jax.sharding import PartitionSpec as P

ITERS = 3
AF = ("af_0", "af_1", "af_2")
R = 128
HALF = 64
INNER = R * R
ROWS = R + 8
K = 10
L = 4
SHARE = K // 2
PACK = SHARE + 5
F32 = jnp.float32
BF16 = jnp.bfloat16
VMEM = pl.BlockSpec(memory_space=pltpu.VMEM)
SMEM = pl.BlockSpec(memory_space=pltpu.SMEM)
HBM = pl.BlockSpec(memory_space=pltpu.HBM)
PARAMS = pltpu.CompilerParams(vmem_limit_bytes=24 << 20)
COST = pl.CostEstimate(flops=10**9, bytes_accessed=10**7, transcendentals=0)


def split(x):
    hi = x.astype(BF16)
    lo = (x - hi.astype(F32)).astype(BF16)
    return hi, lo


def dot3(a, b):
    left = jnp.concatenate([a[0], a[0], a[1]], axis=1)
    right = jnp.concatenate([b[0], b[1], b[0]], axis=0)
    return jnp.dot(left, right, preferred_element_type=F32)


def host_split(x):
    hi = x.astype(np.float32).astype(BF16)
    lo = (x - hi.astype(np.float64)).astype(np.float32).astype(BF16)
    return hi, lo


def first_table(scale):
    dest = np.arange(R)[:, None]
    angle = 2.0 * np.pi * (dest * np.arange(R)[None, :] % R) / R
    real = np.cos(angle)
    imag = -np.sin(angle)
    imag[0] = imag[HALF] = real[HALF]
    real[HALF] = real[0]
    both = [np.concatenate([real[g * HALF :][:HALF], imag[g * HALF :][:HALF]]) for g in (0, 1)]
    return host_split(np.stack(both) * scale)


def last_table():
    angle = 2.0 * np.pi * (np.arange(R)[:, None] * np.arange(R)[None, :] % R) / R
    cos, sin = np.cos(angle), -np.sin(angle)
    return host_split(np.block([[cos, sin], [-sin, cos]]))


def pack_kernel(part_ref, series_hbm, tapers_hbm, out_ref, series_ref, tapers_ref, sems):
    copies = [
        pltpu.make_async_copy(series_hbm, series_ref, sems.at[0]),
        pltpu.make_async_copy(tapers_hbm, tapers_ref, sems.at[1]),
    ]
    for copy in copies:
        copy.start()
    for copy in copies:
        copy.wait()
    total = jnp.zeros((4, R), F32)
    for d in range(R):
        cols = pl.ds(d * R, R)
        x = series_ref[:, cols]
        t = tapers_ref[0:2, cols]
        t = t * t
        total = total + (t[0:1] + t[1:2]) * (x * x)
        out_ref[pl.ds(d * PACK + SHARE, 4), :] = x
    power = jnp.sum(total, axis=1, keepdims=True)
    lane = lax.broadcasted_iota(jnp.int32, (4, R), 1)
    row = lax.broadcasted_iota(jnp.int32, (4, R), 0)
    extra = jnp.sum(jnp.where(lane == row, power, 0.0), axis=0, keepdims=True)
    for d in range(R):
        out_ref[pl.ds(d * PACK + SHARE + 4, 1), :] = extra
    for core in range(2):

        @pl.when(part_ref[2] == core)
        def _():
            for d in range(R):
                share = tapers_ref[core * SHARE : (core + 1) * SHARE, d * R : (d + 1) * R]
                out_ref[pl.ds(d * PACK, SHARE), :] = share


def first_kernel(
    part_ref, got_ref, other_ref, mhi_ref, mlo_ref, out_hbm, power_ref, taper_ref, out_ref, sems
):
    def plane(ref, i):
        return ref[pl.ds(i, R, stride=PACK), :]

    for core in range(2):

        @pl.when(part_ref[2] == core)
        def _():
            for k in range(SHARE):
                taper_ref[core * SHARE + k] = plane(got_ref, k)
                taper_ref[(1 - core) * SHARE + k] = plane(other_ref, k)

    power_ref[...] = jnp.sum(plane(got_ref, SHARE + 4), axis=0, keepdims=True)
    copies = []
    for g in range(2):
        table = (mhi_ref[g], mlo_ref[g])
        for s in range(2):
            x = plane(got_ref, SHARE + 2 * g + s)
            for k in range(0, K, 2):
                y = jnp.concatenate([taper_ref[k] * x, taper_ref[k + 1] * x], axis=1)
                res = dot3(table, split(y))
                for h in range(2):
                    at = g * HALF * 4 * K + s * K + k + h
                    part = res[:, h * R : (h + 1) * R]
                    out_ref[pl.ds(at, HALF, stride=4 * K), :] = part[:HALF]
                    out_ref[pl.ds(at + 2 * K, HALF, stride=4 * K), :] = part[HALF:]
        half = pl.ds(g * HALF * 4 * K, HALF * 4 * K)
        copies.append(pltpu.make_async_copy(out_ref.at[half], out_hbm.at[half], sems.at[g]))
        copies[-1].start()
    for copy in copies:
        copy.wait()


def refine(estimate, variance, powers, conc_ref):
    num = jnp.zeros_like(estimate)
    den = jnp.zeros_like(estimate)
    for k in range(K):
        kept = conc_ref[k]
        base = kept * estimate + (1.0 - kept) * variance
        weight = kept / (base * base)
        num = num + weight * powers[k]
        den = den + weight
    return num / den


def arrange(x, route_ref, turn_ref):
    row = lax.broadcasted_iota(jnp.int32, (R, R), 0)
    col = lax.broadcasted_iota(jnp.int32, (R, R), 1)
    flip = jnp.where(row + col == R - 1, 1.0, 0.0).astype(BF16)
    dot = functools.partial(jnp.dot, preferred_element_type=F32)
    route = route_ref[0 : 2 * R]
    extra = route_ref[2 * R : 2 * R + 16].astype(F32)[0:1]
    own, send = [], []
    last = []
    for i, plane in enumerate(x):
        turned = plane[:R].T
        last.append(plane[R:].T[:, 0:1])
        hi, lo = split(turned)
        turn_ref[:, 2 * i * R : (2 * i + 1) * R] = hi
        turn_ref[:, (2 * i + 1) * R : (2 * i + 2) * R] = lo
    for i in range(len(x)):
        both = turn_ref[:, 2 * i * R : (2 * i + 2) * R]
        back = dot(flip, both).astype(BF16)
        left = [both[:, :R], back[:, :R], both[:, R:], back[:, R:]]
        out = dot(jnp.concatenate(left, axis=1), jnp.concatenate([route, route], axis=0))
        out = out + last[i] * extra
        own.append(out[:, :R])
        send.append(out[:, R:])
    return own, send


def block(b):
    return pl.ds(pl.multiple_of(b * 8, 8), 8)


def counted(estimate, b, special):
    row = b * 8 + lax.broadcasted_iota(jnp.int32, (8, R), 0)
    single = jnp.logical_and(special == 1, jnp.logical_or(row == 0, row == R))
    times = jnp.where(single, 1.0, jnp.where(row < R, 2.0, 0.0))
    return jnp.where(times > 0.0, estimate * times, 0.0)


def share_sums(sums_ref, part_ref, totals):
    lane = lax.broadcasted_iota(jnp.int32, sums_ref.shape, 1)
    out = jnp.zeros(sums_ref.shape, F32)
    for s in range(2):
        out = jnp.where(lane == 2 * part_ref[0] + s, jnp.sum(totals[s]), out)
    sums_ref[...] = out


def read_mean(sums_ref, part_ref, s, scale):
    sums = sums_ref[...]
    lane = lax.broadcasted_iota(jnp.int32, sums.shape, 1)
    return jnp.sum(jnp.where(lane == 2 * part_ref[0] + s, sums, 0.0)) * scale


def second_kernel(
    length_all, part_ref, conc_ref, got_ref, power_ref, w1_ref, tw_ref, last_ref,
    xr_hbm, xi_hbm, powers_hbm, est_ref, sums_ref, xr_ref, xi_ref, powers_ref, sems,
):
    means = [read_mean(power_ref, part_ref, s, 0.5 / length_all) for s in range(2)]
    table = split(w1_ref[...])
    last = (last_ref[0], last_ref[1])
    copies = []
    cos, sin = tw_ref[0], tw_ref[1]

    def plane(i):
        return got_ref[pl.ds(i, R, stride=4 * K), :]

    for a in range(0, 2 * K, 2):
        left = jnp.concatenate([plane(a), plane(2 * K + a)], axis=0)
        right = jnp.concatenate([plane(a + 1), plane(2 * K + a + 1)], axis=0)
        mid = dot3(table, split(jnp.concatenate([left, right], axis=1)))
        rows = []
        for h in range(2):
            re = mid[:ROWS, h * R : (h + 1) * R]
            im = mid[ROWS:, h * R : (h + 1) * R]
            rows.append(jnp.concatenate([re * cos - im * sin, re * sin + im * cos], axis=1))
        out = dot3(split(jnp.concatenate(rows, axis=0)), last)
        for h in range(2):
            re = out[h * ROWS : (h + 1) * ROWS, :R]
            im = out[h * ROWS : (h + 1) * ROWS, R:]
            xr_ref[a + h] = re
            xi_ref[a + h] = im
            powers_ref[a + h] = re * re + im * im
        pair = pl.ds(a, 2)
        for ref, hbm in ((xr_ref, xr_hbm), (xi_ref, xi_hbm), (powers_ref, powers_hbm)):
            sem = sems.at[len(copies)]
            copies.append(pltpu.make_async_copy(ref.at[pair], hbm.at[pair], sem))
            copies[-1].start()

    def rest(b, totals):
        rows = block(b)
        totals = list(totals)
        for s in range(2):
            powers = [powers_ref[s * K + k, rows, :] for k in range(K)]
            estimate = refine(0.5 * (powers[0] + powers[1]), means[s], powers, conc_ref)
            est_ref[s, rows, :] = estimate
            totals[s] = totals[s] + counted(estimate, b, part_ref[1])
        return tuple(totals)

    zero = jnp.zeros((8, R), F32)
    share_sums(sums_ref, part_ref, lax.fori_loop(0, ROWS // 8, rest, (zero, zero)))
    for copy in copies:
        copy.wait()


def inverse_kernel(
    qi_ref, xr_ref, xi_ref, route_ref, own_hbm, send_ref, out_ref, own_ref, pair_ref, turn_ref, sem
):
    at = 0
    for j in range(K):
        for k in range(j, K):
            for l in range(L):
                value = qi_ref[l, j, k]
                value = value if j == k else value + qi_ref[l, k, j]
                pair_ref[at] = jnp.full((8, R), value, F32)
                at += 1

    def step(b, carry):
        rows = block(b)
        re = [xr_ref[i, rows, :] for i in range(2 * K)]
        im = [xi_ref[i, rows, :] for i in range(2 * K)]
        acc = [[None] * L for _ in range(2)]
        at = 0
        for j in range(K):
            for k in range(j, K):
                cross = [
                    re[s * K + j] * re[s * K + k] + im[s * K + j] * im[s * K + k] for s in range(2)
                ]
                for l in range(L):
                    pair = pair_ref[at]
                    at += 1
                    for s in range(2):
                        term = pair * cross[s]
                        acc[s][l] = term if acc[s][l] is None else acc[s][l] + term
        for s in range(2):
            for l in range(L):
                out_ref[s * L + l, rows, :] = acc[s][l]
        return carry

    lax.fori_loop(0, ROWS // 8, step, 0)
    own, send = arrange([out_ref[i] for i in range(2 * L)], route_ref, turn_ref)
    for i in range(2 * L):
        own_ref[i], send_ref[i] = own[i], send[i]
    copy = pltpu.make_async_copy(own_ref, own_hbm, sem)
    copy.start()
    copy.wait()


def refine_kernel(length_all, part_ref, conc_ref, got_ref, powers_ref, est_ref, new_ref, sums_ref):
    means = [read_mean(got_ref, part_ref, s, 1.0 / length_all) for s in range(2)]

    def step(b, totals):
        rows = block(b)
        totals = list(totals)
        for s in range(2):
            powers = [powers_ref[s * K + k, rows, :] for k in range(K)]
            estimate = refine(est_ref[s, rows, :], means[s], powers, conc_ref)
            new_ref[s, rows, :] = estimate
            totals[s] = totals[s] + counted(estimate, b, part_ref[1])
        return tuple(totals)

    zero = jnp.zeros((8, R), F32)
    share_sums(sums_ref, part_ref, lax.fori_loop(0, ROWS // 8, step, (zero, zero)))


def finish_kernel(
    length_all, part_ref, conc_ref, got_ref, powers_ref, est_ref, route_ref, own_ref, send_ref,
    new_ref, turn_ref,
):
    means = [read_mean(got_ref, part_ref, s, 1.0 / length_all) for s in range(2)]

    def step(b, carry):
        rows = block(b)
        for s in range(2):
            powers = [powers_ref[s * K + k, rows, :] for k in range(K)]
            new_ref[s, rows, :] = refine(est_ref[s, rows, :], means[s], powers, conc_ref)
        return carry

    lax.fori_loop(0, ROWS // 8, step, 0)
    own, send = arrange([new_ref[s] for s in range(2)], route_ref, turn_ref)
    for s in range(2):
        own_ref[s], send_ref[s] = own[s], send[s]


def merge_kernel(part_ref, mine_ref, theirs_ref, out_ref):
    half = mine_ref.shape[0]
    for g in range(2):

        @pl.when(part_ref[0] == g)
        def _():
            out_ref[g * half : (g + 1) * half] = mine_ref[...]
            out_ref[(1 - g) * half : (2 - g) * half] = theirs_ref[...]


def in_hbm(x):
    return pltpu.with_memory_space_constraint(x, pltpu.HBM)


def exchange(x):
    return lax.all_to_all(x, AF, split_axis=0, concat_axis=0, tiled=True)


def tables(q, special, length_all):
    row = lax.broadcasted_iota(jnp.int32, (ROWS, R), 0)
    col = lax.broadcasted_iota(jnp.int32, (ROWS, R), 1)
    upper = jnp.logical_and(row >= HALF, row < R)
    halves = jnp.where(row < HALF, R * row, jnp.where(row < R, R * (row - HALF) + HALF, R * HALF))
    phase = col * jnp.where(special, halves, R * row + q)
    angle = (phase % INNER).astype(F32) * (2.0 * math.pi / INNER)
    re, im = jnp.cos(angle), -jnp.sin(angle)
    ordinary = jnp.logical_and(jnp.logical_not(special), row < R)
    from_imag = jnp.logical_and(special, upper)
    from_real = jnp.logical_or(
        ordinary, jnp.logical_and(special, jnp.logical_or(row < HALF, row == R))
    )
    a = jnp.where(from_real, re, 0.0)
    c = jnp.where(from_real, im, 0.0)
    b = jnp.where(ordinary, -im, jnp.where(from_imag, re, 0.0))
    d = jnp.where(ordinary, re, jnp.where(from_imag, im, 0.0))
    first = jnp.concatenate([jnp.concatenate([a, b], axis=1), jnp.concatenate([c, d], axis=1)])
    angle = phase.astype(F32) * (2.0 * math.pi / length_all)
    return first, jnp.stack([jnp.cos(angle), -jnp.sin(angle)])


def route_table(q, special):
    row = lax.broadcasted_iota(jnp.int32, (2 * R + 16, 2 * R), 0)
    col = lax.broadcasted_iota(jnp.int32, (2 * R + 16, 2 * R), 1)
    c = col % R
    send = col >= R
    row_0 = jnp.where(c < HALF, c, jnp.where(c == HALF, 2 * R, R + R - c))
    row_64 = jnp.where(c < HALF, HALF + c, R + HALF + R - 1 - c)
    plain = jnp.where(send, R + R - 1 - c, c)
    source = jnp.where(special, jnp.where(send == (q == 0), row_64, row_0), plain)
    return (row == source).astype(BF16)


def local(series, tapers, concentration, qi_weights):
    length_all = series.shape[1] * R
    q = lax.axis_index(AF)
    group = (q >= HALF).astype(jnp.int32)
    special = (q % HALF) == 0
    part = jnp.stack([group, special.astype(jnp.int32), lax.axis_index("sa")])
    shape = jax.ShapeDtypeStruct

    packed = pl.pallas_call(
        pack_kernel,
        out_shape=shape((R * PACK, R), F32),
        in_specs=[SMEM, HBM, HBM],
        out_specs=VMEM,
        scratch_shapes=[
            pltpu.VMEM(series.shape, F32),
            pltpu.VMEM(tapers.shape, F32),
            pltpu.SemaphoreType.DMA((2,)),
        ],
        name="pack",
        compiler_params=PARAMS,
    )(part, in_hbm(series), in_hbm(tapers))
    got = exchange(packed.reshape(R, PACK * R)).reshape(R * PACK, R)
    other = lax.ppermute(got, "sa", [(0, 1), (1, 0)])

    first, tw = tables(q, special, length_all)
    route = route_table(q, special)
    mhi, mlo = first_table(1.0 / math.sqrt(length_all))
    spread, power = pl.pallas_call(
        first_kernel,
        out_shape=(pltpu.HBM((R * 4 * K, R), F32), shape((1, R), F32)),
        in_specs=[SMEM] + [VMEM] * 4,
        out_specs=(HBM, VMEM),
        scratch_shapes=[
            pltpu.VMEM((K, R, R), F32),
            pltpu.VMEM((R * 4 * K, R), F32),
            pltpu.SemaphoreType.DMA((2,)),
        ],
        name="first",
        compiler_params=PARAMS,
    )(part, got, other, jnp.asarray(mhi), jnp.asarray(mlo))
    got = exchange(spread.reshape(R, 4 * K, R)).reshape(R * 4 * K, R)

    spectra = shape((2 * K, ROWS, R), F32)
    estimates = shape((2, ROWS, R), F32)
    totals = shape((R, 8), F32)
    xr, xi, powers, est, sums = pl.pallas_call(
        functools.partial(second_kernel, length_all),
        out_shape=(pltpu.HBM(spectra.shape, F32),) * 3 + (estimates, totals),
        in_specs=[SMEM] * 2 + [VMEM] * 5,
        out_specs=(HBM,) * 3 + (VMEM,) * 2,
        scratch_shapes=[pltpu.VMEM(spectra.shape, F32)] * 3 + [pltpu.SemaphoreType.DMA((3 * K,))],
        name="second",
        compiler_params=PARAMS,
    )(part, concentration, got, power, first, tw, jnp.asarray(np.stack(last_table())))

    sums = exchange(sums)
    parts = (2 * L, R, R)
    own_qi, send_qi = pl.pallas_call(
        inverse_kernel,
        out_shape=(pltpu.HBM(parts, F32), shape(parts, F32)),
        in_specs=[SMEM] + [VMEM] * 3,
        out_specs=(HBM, VMEM),
        scratch_shapes=[
            pltpu.VMEM((2 * L, ROWS, R), F32),
            pltpu.VMEM(parts, F32),
            pltpu.VMEM((L * K * (K + 1) // 2, 8, R), F32),
            pltpu.VMEM((R, 4 * L * R), BF16),
            pltpu.SemaphoreType.DMA,
        ],
        cost_estimate=COST,
        name="inverse",
        compiler_params=PARAMS,
    )(qi_weights, xr, xi, route)

    partner = [(i, HALF - i if i % HALF == 0 else R - i) for i in range(R)]
    sums, own_qi, send_qi = lax.optimization_barrier((sums, own_qi, send_qi))
    got_qi = lax.ppermute(send_qi, AF, partner)
    est, sums = pl.pallas_call(
        functools.partial(refine_kernel, length_all),
        out_shape=(estimates, totals),
        in_specs=[SMEM] * 2 + [VMEM] * 3,
        out_specs=(VMEM,) * 2,
        name="refine",
        compiler_params=PARAMS,
    )(part, concentration, sums, powers, est)

    sums = exchange(sums)
    parts = shape((2, R, R), F32)
    own, send = pl.pallas_call(
        functools.partial(finish_kernel, length_all),
        out_shape=(parts, parts),
        in_specs=[SMEM] * 2 + [VMEM] * 4,
        out_specs=(VMEM,) * 2,
        scratch_shapes=[pltpu.VMEM((2, ROWS, R), F32), pltpu.VMEM((R, 4 * R), BF16)],
        name="finish",
        compiler_params=PARAMS,
    )(part, concentration, sums, powers, est, route)
    got_est = lax.ppermute(send, AF, partner)

    def merge(mine, theirs):
        return pl.pallas_call(
            merge_kernel,
            out_shape=shape((2 * mine.shape[0], R, R), F32),
            in_specs=[SMEM] + [VMEM] * 2,
            out_specs=VMEM,
            name="merge",
            compiler_params=PARAMS,
        )(part, mine, theirs)

    own, own_qi = lax.optimization_barrier((own, own_qi))
    qi_out = merge(own_qi, got_qi)
    return merge(own, got_est).reshape(4, 1, INNER), qi_out.reshape(4, L, 1, INNER)


def solution(mesh):
    torus = Mesh(mesh.devices.reshape(4, 4, 8, mesh.shape["sa"]), AF + ("sa",))
    in_specs = (P("sa", AF), P(None, AF), P(), P())
    out_specs = (P("sa", AF, None), P("sa", None, AF, None))
    return jax.shard_map(local, mesh=torus, in_specs=in_specs, out_specs=out_specs, check_vma=False)
```
